512 devices in a mesh: row: 16 (over z), col: 16 (over y, x_lo, core), depth: 2 (over x_hi).
Axes of the slice: x: 4 (x_hi: 2, x_lo: 2; x = x_hi * 2 + x_lo), y: 4, z: 16, core: 2. Of those that a mesh axis runs over, the one named last changes fastest.
Arguments:
- amplitudes: float32 [3072, 11520], P('row', ('col', 'depth')), may hold values from -6 to 6
- integrals: float32 [11520, 5760], P(('row', 'depth'), 'col'), may hold values from -0.0546875 to 0.0546875
Outputs:
- ladder: float32 [3072, 5760], P(('row', 'depth'), 'col')
The draws below stay inside these ranges and needn't reach their ends.
All inputs are finite; a program needn't handle non-finite values.
Results may differ from the reference program's by a relative error of at most 0.00007.
Values sent between devices are 32-bit elements; how exact they have to be, the bound alone decides.
No kernel may reach another device: no remote copies, remote signals or barrier semaphores. Data moves between devices by JAX's collectives and lax.ppermute only.
A program may use at most 64 MiB of HBM per device.

```python
import jax
import jax.numpy as jnp
from jax import lax

KCD = 11520
NAB = 5760
PAIRS = 3072


def levels(rng, extent, pieces, low, top_value):
    factor_of = 1.0
    for axis_at, blocks in pieces:
        steps = jax.random.uniform(jax.random.fold_in(jax.random.fold_in(rng, 6), axis_at), (blocks,), jnp.float32, low / len(pieces), top_value / len(pieces))
        factor_of = factor_of * jnp.repeat(jnp.exp(steps), extent[axis_at] // blocks).reshape((-1,) + (1,) * (len(extent) - 1 - axis_at))
    return factor_of


def centred(key, dims, deviation, bound, split=(), kind=jnp.bfloat16):
    factor_of = levels(key, dims, split, -0.22, 0.18) if split else 1.0
    result = jax.random.normal(key, dims, jnp.float32) * deviation * factor_of
    return jnp.minimum(jnp.maximum(result, -bound), bound).astype(kind)


def setup_inputs(seed: int = 0) -> dict:
    splits = jax.random.split(jax.random.key(seed), 3)
    return {
        "amplitudes": centred(splits[0], (PAIRS, KCD), 1.0, 6.0, ((0, 16), (1, 32)), jnp.float32),
        "integrals": centred(splits[1], (KCD, NAB), KCD ** -0.5, 0.0546875, ((0, 32), (1, 16)), jnp.float32),
    }


def reference(amplitudes, integrals):
    product = jnp.dot(amplitudes, integrals, precision=lax.Precision.HIGHEST, preferred_element_type=jnp.float32)
    return 0.5 * product
```

```python
import jax
import jax.numpy as jnp
from jax import lax
from jax.sharding import PartitionSpec as P


def local(amplitudes, integrals):
    n = lax.axis_size("row")
    me = lax.axis_index("row")
    d = lax.axis_index("depth")
    kb = integrals.shape[0]
    rows = amplitudes.shape[0]
    half = rows // 2

    strip = lax.all_gather(amplitudes, "col", axis=1, tiled=True)

    def product(block, owner):
        cols = lax.dynamic_slice_in_dim(strip, owner * kb, kb, axis=1)
        return jnp.dot(cols, block, precision=lax.Precision.HIGHEST,
                       preferred_element_type=jnp.float32)

    fwd = [(i, (i + 1) % n) for i in range(n)]
    bwd = [(i, (i - 1) % n) for i in range(n)]
    total = product(integrals, me)
    ahead = integrals
    behind = integrals
    for step in range(1, n // 2 + 1):
        ahead = lax.ppermute(ahead, "row", fwd)
        total = total + product(ahead, (me - step) % n)
        if step < n - n // 2:
            behind = lax.ppermute(behind, "row", bwd)
            total = total + product(behind, (me + step) % n)

    mine = lax.dynamic_slice_in_dim(total, d * half, half, axis=0)
    other = lax.dynamic_slice_in_dim(total, (1 - d) * half, half, axis=0)
    other = lax.ppermute(other, "depth", [(0, 1), (1, 0)])
    return 0.5 * (mine + other)


def solution(mesh):
    placed = (P("row", ("col", "depth")), P(("row", "depth"), "col"))
    return jax.shard_map(
        local, mesh=mesh, in_specs=placed, out_specs=P(("row", "depth"), "col"), check_vma=False
    )
```

```python
import jax
import jax.numpy as jnp
from jax import lax
from jax.sharding import PartitionSpec as P


FIRST_DOT_STEP = 4
DOTS_PER_STEP = 5


def local(amplitudes, integrals):
    n = lax.axis_size("row")
    me = lax.axis_index("row")
    d = lax.axis_index("depth")
    kb = integrals.shape[0]
    rows = amplitudes.shape[0]
    half = rows // 2

    strip = lax.all_gather(amplitudes, "col", axis=0, tiled=False)

    def product(block, owner):
        cols = lax.dynamic_index_in_dim(strip, owner, axis=0, keepdims=False)
        return jnp.dot(cols, block, precision=lax.Precision.HIGHEST,
                       preferred_element_type=jnp.float32)

    fwd = [(i, (i + 1) % n) for i in range(n)]
    bwd = [(i, (i - 1) % n) for i in range(n)]
    total = None
    pending = [(integrals, me)]
    ahead = integrals
    behind = integrals
    for step in range(1, n // 2 + 1):
        arrived = []
        ahead = lax.ppermute(ahead, "row", fwd)
        arrived.append((ahead, (me - step) % n))
        if step < n - n // 2:
            behind = lax.ppermute(behind, "row", bwd)
            arrived.append((behind, (me + step) % n))
        if step >= FIRST_DOT_STEP:
            for block, owner in pending[:DOTS_PER_STEP]:
                part = product(block, owner)
                total = part if total is None else total + part
            pending = pending[DOTS_PER_STEP:]
            total, ahead, behind = lax.optimization_barrier((total, ahead, behind))
        pending = pending + arrived
    for block, owner in pending:
        part = product(block, owner)
        total = part if total is None else total + part

    mine = lax.dynamic_slice_in_dim(total, d * half, half, axis=0)
    other = lax.dynamic_slice_in_dim(total, (1 - d) * half, half, axis=0)
    other = lax.ppermute(other, "depth", [(0, 1), (1, 0)])
    return 0.5 * (mine + other)


def solution(mesh):
    placed = (P("row", ("col", "depth")), P(("row", "depth"), "col"))
    return jax.shard_map(
        local, mesh=mesh, in_specs=placed, out_specs=P(("row", "depth"), "col"), check_vma=False
    )
```

```python
import jax
import jax.numpy as jnp
from jax import lax
from jax.sharding import PartitionSpec as P


def local(amplitudes, integrals):
    n = lax.axis_size("row")
    swap = [(i * n + c, c * n + i) for i in range(n) for c in range(n)]
    moved = lax.ppermute(amplitudes, ("row", "col"), swap)
    strip = lax.all_gather(moved, "col", axis=0, tiled=True)
    partial = jnp.dot(strip, integrals, precision=lax.Precision.HIGHEST,
                      preferred_element_type=jnp.float32)
    total = lax.psum_scatter(partial, ("row", "depth"), scatter_dimension=0, tiled=True)
    return 0.5 * total


def solution(mesh):
    placed = (P("row", ("col", "depth")), P(("row", "depth"), "col"))
    return jax.shard_map(
        local, mesh=mesh, in_specs=placed, out_specs=P(("row", "depth"), "col"), check_vma=False
    )
```

```python
import jax
import jax.numpy as jnp
from jax import lax
from jax.sharding import PartitionSpec as P

FIRST_DOT_STEP = 5
DOTS_PER_STEP = 5


def gather_col(block):
    n = lax.axis_size("col")
    c = lax.axis_index("col")
    core, xlo, y = c % 2, (c // 2) % 2, c // 4
    ny = n // 4
    other = lax.ppermute(block, "col", [(i, i ^ 1) for i in range(n)])
    pair = jnp.where(core == 0, jnp.stack([block, other]), jnp.stack([other, block]))
    far = lax.ppermute(pair, "col", [(i, i ^ 2) for i in range(n)])
    quad = jnp.where(xlo == 0, jnp.concatenate([pair, far]), jnp.concatenate([far, pair]))
    up = [(i, (i + 4) % n) for i in range(n)]
    down = [(i, (i - 4) % n) for i in range(n)]
    below = lax.ppermute(quad, "col", up)
    above = lax.ppermute(quad, "col", down)
    h = quad.shape[1] // 2
    opp_a = lax.ppermute(below[:, :h], "col", up)
    opp_b = lax.ppermute(above[:, h:], "col", down)
    opposite = jnp.concatenate([opp_a, opp_b], axis=1)
    stack = jnp.concatenate([quad, above, opposite, below])

    def place(owner):
        return ((owner // 4 - y) % ny) * 4 + owner % 4

    return stack, place


def local(amplitudes, integrals):
    n = lax.axis_size("row")
    me = lax.axis_index("row")
    d = lax.axis_index("depth")
    kb = integrals.shape[0]
    rows = amplitudes.shape[0]
    half = rows // 2

    strip, place = gather_col(amplitudes)

    def product(block, owner, lo=0, hi=None):
        hi = kb if hi is None else hi
        cols = lax.dynamic_index_in_dim(strip, place(owner), axis=0, keepdims=False)
        return jnp.dot(cols[:, lo:hi], block, precision=lax.Precision.HIGHEST,
                       preferred_element_type=jnp.float32)

    fwd = [(i, (i + 1) % n) for i in range(n)]
    bwd = [(i, (i - 1) % n) for i in range(n)]
    total = None
    pending = [(integrals, me, 0, kb)]
    ahead = integrals
    behind = integrals
    last = n // 2
    for step in range(1, last + 1):
        arrived = []
        if step < last:
            ahead = lax.ppermute(ahead, "row", fwd)
            arrived.append((ahead, (me - step) % n, 0, kb))
            behind = lax.ppermute(behind, "row", bwd)
            arrived.append((behind, (me + step) % n, 0, kb))
        else:
            m = kb // 2
            top = lax.ppermute(ahead[:m], "row", fwd)
            bottom = lax.ppermute(behind[m:], "row", bwd)
            arrived.append((top, (me - step) % n, 0, m))
            arrived.append((bottom, (me - step) % n, m, kb))
            ahead, behind = top, bottom
        if step >= FIRST_DOT_STEP:
            for block, owner, lo, hi in pending[:DOTS_PER_STEP]:
                part = product(block, owner, lo, hi)
                total = part if total is None else total + part
            pending = pending[DOTS_PER_STEP:]
            total, ahead, behind = lax.optimization_barrier((total, ahead, behind))
        pending = pending + arrived
    for block, owner, lo, hi in pending:
        part = product(block, owner, lo, hi)
        total = part if total is None else total + part

    mine = lax.dynamic_slice_in_dim(total, d * half, half, axis=0)
    other = lax.dynamic_slice_in_dim(total, (1 - d) * half, half, axis=0)
    other = lax.ppermute(other, "depth", [(0, 1), (1, 0)])
    return 0.5 * (mine + other)


def solution(mesh):
    placed = (P("row", ("col", "depth")), P(("row", "depth"), "col"))
    return jax.shard_map(
        local, mesh=mesh, in_specs=placed, out_specs=P(("row", "depth"), "col"), check_vma=False
    )
```

```python
import jax
import jax.numpy as jnp
from jax import lax
from jax.sharding import PartitionSpec as P

CHUNKS = 4


def gather_col(block):
    n = lax.axis_size("col")
    c = lax.axis_index("col")
    core, xlo, y = c % 2, (c // 2) % 2, c // 4
    ny = n // 4
    other = lax.ppermute(block, "col", [(i, i ^ 1) for i in range(n)])
    pair = jnp.where(core == 0, jnp.stack([block, other]), jnp.stack([other, block]))
    far = lax.ppermute(pair, "col", [(i, i ^ 2) for i in range(n)])
    quad = jnp.where(xlo == 0, jnp.concatenate([pair, far]), jnp.concatenate([far, pair]))
    up = [(i, (i + 4) % n) for i in range(n)]
    down = [(i, (i - 4) % n) for i in range(n)]
    below = lax.ppermute(quad, "col", up)
    above = lax.ppermute(quad, "col", down)
    h = quad.shape[1] // 2
    opp_a = lax.ppermute(below[:, :h], "col", up)
    opp_b = lax.ppermute(above[:, h:], "col", down)
    opposite = jnp.concatenate([opp_a, opp_b], axis=1)
    stack = jnp.concatenate([quad, above, opposite, below])

    def place(owner):
        return ((owner // 4 - y) % ny) * 4 + owner % 4

    return stack, place


def local(amplitudes, integrals):
    d = lax.axis_index("depth")
    rows = amplitudes.shape[0]
    half = rows // 2
    width = integrals.shape[1]

    stack, place = gather_col(amplitudes)
    n = stack.shape[0]
    order = jnp.stack([place(jnp.int32(k)) for k in range(n)])
    strip = jnp.take(stack, order, axis=0)

    outs = []
    step = width // CHUNKS
    for k in range(CHUNKS):
        piece = lax.all_gather(integrals[:, k * step:(k + 1) * step], "row", axis=0, tiled=False)
        total = lax.dot_general(strip, piece, (((0, 2), (0, 1)), ((), ())),
                                precision=lax.Precision.HIGHEST,
                                preferred_element_type=jnp.float32)
        mine = lax.dynamic_slice_in_dim(total, d * half, half, axis=0)
        other = lax.dynamic_slice_in_dim(total, (1 - d) * half, half, axis=0)
        other = lax.ppermute(other, "depth", [(0, 1), (1, 0)])
        outs.append(0.5 * (mine + other))
    return jnp.concatenate(outs, axis=1)


def solution(mesh):
    placed = (P("row", ("col", "depth")), P(("row", "depth"), "col"))
    return jax.shard_map(
        local, mesh=mesh, in_specs=placed, out_specs=P(("row", "depth"), "col"), check_vma=False
    )
```

```python
import functools

import jax
import jax.numpy as jnp
from jax import lax
from jax.experimental import pallas as pl
from jax.experimental.pallas import tpu as pltpu
from jax.sharding import PartitionSpec as P

FIRST_DOT_STEP = 5
DOTS_PER_STEP = 5
SHARE = 180


def gather_col(block):
    n = lax.axis_size("col")
    c = lax.axis_index("col")
    core, xlo, y = c % 2, (c // 2) % 2, c // 4
    ny = n // 4
    other = lax.ppermute(block, "col", [(i, i ^ 1) for i in range(n)])
    pair = jnp.where(core == 0, jnp.stack([block, other]), jnp.stack([other, block]))
    far = lax.ppermute(pair, "col", [(i, i ^ 2) for i in range(n)])
    quad = jnp.where(xlo == 0, jnp.concatenate([pair, far]), jnp.concatenate([far, pair]))
    up = [(i, (i + 4) % n) for i in range(n)]
    down = [(i, (i - 4) % n) for i in range(n)]
    below = lax.ppermute(quad, "col", up)
    above = lax.ppermute(quad, "col", down)
    h = quad.shape[1] // 2
    opp_a = lax.ppermute(below[:, :h], "col", up)
    opp_b = lax.ppermute(above[:, h:], "col", down)
    opposite = jnp.concatenate([opp_a, opp_b], axis=1)
    stack = jnp.concatenate([quad, above, opposite, below])

    def place(owner):
        return ((owner // 4 - y) % ny) * 4 + owner % 4

    return stack, place


def _stacked_kernel(share, places, a_ref, b_ref, o_ref):
    @pl.when(pl.program_id(0) == 0)
    def _():
        o_ref[...] = jnp.zeros_like(o_ref)

    a = a_ref[0, :, :share]
    o_ref[...] += jnp.dot(a, b_ref[0], precision=lax.Precision.HIGHEST,
                          preferred_element_type=jnp.float32)


def stacked_product(places, stack, gathered):
    n, rows, kb = stack.shape
    share, width = gathered.shape[1], gathered.shape[2]
    grid_spec = pltpu.PrefetchScalarGridSpec(
        num_scalar_prefetch=1,
        grid=(n,),
        in_specs=[
            pl.BlockSpec((1, rows, kb), lambda b, pr: (pr[b], 0, 0)),
            pl.BlockSpec((1, share, width), lambda b, pr: (b, 0, 0)),
        ],
        out_specs=pl.BlockSpec((rows, width), lambda b, pr: (0, 0)),
    )
    return pl.pallas_call(
        functools.partial(_stacked_kernel, share),
        grid_spec=grid_spec,
        out_shape=jax.ShapeDtypeStruct((rows, width), jnp.float32),
    )(places, stack, gathered)


def local(amplitudes, integrals):
    n = lax.axis_size("row")
    me = lax.axis_index("row")
    d = lax.axis_index("depth")
    kb = integrals.shape[0] - SHARE
    rows = amplitudes.shape[0]
    half = rows // 2

    strip, place = gather_col(amplitudes)
    upper = lax.all_gather(integrals[:SHARE], "row", axis=0, tiled=False)
    places = jnp.stack([place(jnp.int32(k)) for k in range(n)]).astype(jnp.int32)
    integrals = integrals[SHARE:]

    def product(block, owner, lo=0, hi=None):
        hi = kb if hi is None else hi
        cols = lax.dynamic_index_in_dim(strip, place(owner), axis=0, keepdims=False)
        return jnp.dot(cols[:, SHARE + lo:SHARE + hi], block, precision=lax.Precision.HIGHEST,
                       preferred_element_type=jnp.float32)

    fwd = [(i, (i + 1) % n) for i in range(n)]
    bwd = [(i, (i - 1) % n) for i in range(n)]
    total = None
    pending = [(integrals, me, 0, kb)]
    ahead = integrals
    behind = integrals
    last = n // 2
    for step in range(1, last + 1):
        arrived = []
        if step < last:
            ahead = lax.ppermute(ahead, "row", fwd)
            arrived.append((ahead, (me - step) % n, 0, kb))
            behind = lax.ppermute(behind, "row", bwd)
            arrived.append((behind, (me + step) % n, 0, kb))
        else:
            m = kb // 2
            top = lax.ppermute(ahead[:m], "row", fwd)
            bottom = lax.ppermute(behind[m:], "row", bwd)
            arrived.append((top, (me - step) % n, 0, m))
            arrived.append((bottom, (me - step) % n, m, kb))
            ahead, behind = top, bottom
        if step >= FIRST_DOT_STEP:
            for block, owner, lo, hi in pending[:DOTS_PER_STEP]:
                part = product(block, owner, lo, hi)
                total = part if total is None else total + part
            pending = pending[DOTS_PER_STEP:]
            total, ahead, behind = lax.optimization_barrier((total, ahead, behind))
        pending = pending + arrived
    for block, owner, lo, hi in pending:
        part = product(block, owner, lo, hi)
        total = part if total is None else total + part

    total = total + stacked_product(places, strip, upper)
    mine = lax.dynamic_slice_in_dim(total, d * half, half, axis=0)
    other = lax.dynamic_slice_in_dim(total, (1 - d) * half, half, axis=0)
    other = lax.ppermute(other, "depth", [(0, 1), (1, 0)])
    return 0.5 * (mine + other)


def solution(mesh):
    placed = (P("row", ("col", "depth")), P(("row", "depth"), "col"))
    return jax.shard_map(
        local, mesh=mesh, in_specs=placed, out_specs=P(("row", "depth"), "col"), check_vma=False
    )
```

```python
import functools

import jax
import jax.numpy as jnp
from jax import lax
from jax.experimental import pallas as pl
from jax.experimental.pallas import tpu as pltpu
from jax.sharding import PartitionSpec as P

FIRST_DOT_STEP = 5
DOTS_PER_STEP = 5


def gather_col(block):
    n = lax.axis_size("col")
    c = lax.axis_index("col")
    core, xlo, y = c % 2, (c // 2) % 2, c // 4
    ny = n // 4
    other = lax.ppermute(block, "col", [(i, i ^ 1) for i in range(n)])
    pair = jnp.where(core == 0, jnp.stack([block, other]), jnp.stack([other, block]))
    far = lax.ppermute(pair, "col", [(i, i ^ 2) for i in range(n)])
    quad = jnp.where(xlo == 0, jnp.concatenate([pair, far]), jnp.concatenate([far, pair]))
    up = [(i, (i + 4) % n) for i in range(n)]
    down = [(i, (i - 4) % n) for i in range(n)]
    below = lax.ppermute(quad, "col", up)
    above = lax.ppermute(quad, "col", down)
    h = quad.shape[1] // 2
    opp_a = lax.ppermute(below[:, :h], "col", up)
    opp_b = lax.ppermute(above[:, h:], "col", down)
    opposite = jnp.concatenate([opp_a, opp_b], axis=1)
    stack = jnp.concatenate([quad, above, opposite, below])

    def place(owner):
        return ((owner // 4 - y) % ny) * 4 + owner % 4

    return stack, place


def _accumulate_kernel(lo, hi, first, place_ref, a_ref, b_ref, *refs):
    o_ref = refs[-1]
    part = jnp.dot(a_ref[0, :, lo:hi], b_ref[...], precision=lax.Precision.HIGHEST,
                   preferred_element_type=jnp.float32)
    if first:
        o_ref[...] = part
    else:
        o_ref[...] = refs[0][...] + part


def accumulate(total, stack, block, where, lo, hi):
    _, rows, kb = stack.shape
    width = block.shape[1]
    first = total is None
    in_specs = [
        pl.BlockSpec((1, rows, kb), lambda i, pr: (pr[0], 0, 0)),
        pl.BlockSpec(block.shape, lambda i, pr: (0, 0)),
    ]
    args = [stack, block]
    if not first:
        in_specs.append(pl.BlockSpec((rows, width), lambda i, pr: (0, 0)))
        args.append(total)
    grid_spec = pltpu.PrefetchScalarGridSpec(
        num_scalar_prefetch=1,
        grid=(1,),
        in_specs=in_specs,
        out_specs=pl.BlockSpec((rows, width), lambda i, pr: (0, 0)),
    )
    return pl.pallas_call(
        functools.partial(_accumulate_kernel, lo, hi, first),
        grid_spec=grid_spec,
        out_shape=jax.ShapeDtypeStruct((rows, width), jnp.float32),
        input_output_aliases={} if first else {3: 0},
    )(jnp.reshape(where, (1,)).astype(jnp.int32), *args)


def local(amplitudes, integrals):
    n = lax.axis_size("row")
    me = lax.axis_index("row")
    d = lax.axis_index("depth")
    kb = integrals.shape[0]
    rows = amplitudes.shape[0]
    half = rows // 2

    strip, place = gather_col(amplitudes)


    fwd = [(i, (i + 1) % n) for i in range(n)]
    bwd = [(i, (i - 1) % n) for i in range(n)]
    total = None
    pending = [(integrals, me, 0, kb)]
    ahead = integrals
    behind = integrals
    last = n // 2
    for step in range(1, last + 1):
        arrived = []
        if step < last:
            ahead = lax.ppermute(ahead, "row", fwd)
            arrived.append((ahead, (me - step) % n, 0, kb))
            behind = lax.ppermute(behind, "row", bwd)
            arrived.append((behind, (me + step) % n, 0, kb))
        else:
            m = kb // 2
            top = lax.ppermute(ahead[:m], "row", fwd)
            bottom = lax.ppermute(behind[m:], "row", bwd)
            arrived.append((top, (me - step) % n, 0, m))
            arrived.append((bottom, (me - step) % n, m, kb))
            ahead, behind = top, bottom
        if step >= FIRST_DOT_STEP:
            for block, owner, lo, hi in pending[:DOTS_PER_STEP]:
                total = accumulate(total, strip, block, place(owner), lo, hi)
            pending = pending[DOTS_PER_STEP:]
            total, ahead, behind = lax.optimization_barrier((total, ahead, behind))
        pending = pending + arrived
    for block, owner, lo, hi in pending:
        total = accumulate(total, strip, block, place(owner), lo, hi)

    mine = lax.dynamic_slice_in_dim(total, d * half, half, axis=0)
    other = lax.dynamic_slice_in_dim(total, (1 - d) * half, half, axis=0)
    other = lax.ppermute(other, "depth", [(0, 1), (1, 0)])
    return 0.5 * (mine + other)


def solution(mesh):
    placed = (P("row", ("col", "depth")), P(("row", "depth"), "col"))
    return jax.shard_map(
        local, mesh=mesh, in_specs=placed, out_specs=P(("row", "depth"), "col"), check_vma=False
    )
```

```python
import jax
import jax.numpy as jnp
from jax import lax
from jax.sharding import PartitionSpec as P


def ring_reduce(gathered, integrals, me, n):
    fwd = [(i, (i + 1) % n) for i in range(n)]
    bwd = [(i, (i - 1) % n) for i in range(n)]

    def part(t):
        block = lax.dynamic_index_in_dim(gathered, t % n, axis=0, keepdims=False)
        return jnp.dot(block, integrals, precision=lax.Precision.HIGHEST,
                       preferred_element_type=jnp.float32)

    back = n // 2
    ahead = n - 1 - back
    acc_f = part(me + ahead)
    acc_b = part(me - back)
    for s in range(1, back + 1):
        if s <= ahead:
            acc_f = lax.ppermute(acc_f, "row", fwd) + part(me + ahead - s)
        got = lax.ppermute(acc_b, "row", bwd)
        acc_b = got + part(me - back + s) if s < back else got
    return acc_f + acc_b


def local(amplitudes, integrals):
    n = lax.axis_size("row")
    me = lax.axis_index("row")
    d = lax.axis_index("depth")
    rows = amplitudes.shape[0]
    half = rows // 2

    swap = [(i * n + c, c * n + i) for i in range(n) for c in range(n)]
    moved = lax.ppermute(amplitudes, ("row", "col"), swap)
    theirs = lax.dynamic_slice_in_dim(moved, (1 - d) * half, half, axis=0)
    mine = lax.dynamic_slice_in_dim(moved, d * half, half, axis=0)
    g_theirs = lax.all_gather(theirs, "col", axis=0, tiled=False)
    g_mine = lax.all_gather(mine, "col", axis=0, tiled=False)

    sent = ring_reduce(g_theirs, integrals, me, n)
    got = lax.ppermute(sent, "depth", [(0, 1), (1, 0)])
    own = ring_reduce(g_mine, integrals, me, n)
    return 0.5 * (own + got)


def solution(mesh):
    placed = (P("row", ("col", "depth")), P(("row", "depth"), "col"))
    return jax.shard_map(
        local, mesh=mesh, in_specs=placed, out_specs=P(("row", "depth"), "col"), check_vma=False
    )
```

```python
import jax
import jax.numpy as jnp
from jax import lax
from jax.sharding import PartitionSpec as P

FIRST_DOT_STEP = 5
DOTS_PER_STEP = 2


def gather_col(block):
    n = lax.axis_size("col")
    c = lax.axis_index("col")
    core, xlo, y = c % 2, (c // 2) % 2, c // 4
    ny = n // 4
    other = lax.ppermute(block, "col", [(i, i ^ 1) for i in range(n)])
    pair = jnp.where(core == 0, jnp.stack([block, other]), jnp.stack([other, block]))
    far = lax.ppermute(pair, "col", [(i, i ^ 2) for i in range(n)])
    quad = jnp.where(xlo == 0, jnp.concatenate([pair, far]), jnp.concatenate([far, pair]))
    up = [(i, (i + 4) % n) for i in range(n)]
    down = [(i, (i - 4) % n) for i in range(n)]
    below = lax.ppermute(quad, "col", up)
    above = lax.ppermute(quad, "col", down)
    h = quad.shape[1] // 2
    opp_a = lax.ppermute(below[:, :h], "col", up)
    opp_b = lax.ppermute(above[:, h:], "col", down)
    opposite = jnp.concatenate([opp_a, opp_b], axis=1)
    stack = jnp.concatenate([quad, above, opposite, below])

    def place(owner):
        return ((owner // 4 - y) % ny) * 4 + owner % 4

    return stack, place


def local(amplitudes, integrals):
    n = lax.axis_size("row")
    m = lax.axis_size("col")
    me = lax.axis_index("row")
    d = lax.axis_index("depth")
    core = lax.axis_index("col") % 2
    kb = integrals.shape[0]
    rows = amplitudes.shape[0]
    half = rows // 2
    sign = 2 * core - 1

    strip, place = gather_col(amplitudes)

    def cols(owner):
        return lax.dynamic_index_in_dim(strip, place(owner % n), axis=0, keepdims=False)

    def dot(a, b):
        return jnp.dot(a, b, precision=lax.Precision.HIGHEST,
                       preferred_element_type=jnp.float32)

    partner = lax.ppermute(integrals, "col", [(i, i ^ 1) for i in range(m)])
    pair = jnp.where(core == 0, jnp.stack([integrals, partner]),
                     jnp.stack([partner, integrals]))
    ring = [(r * m + c, ((r + 1 - 2 * (c % 2)) % n) * m + c)
            for r in range(n) for c in range(m)]

    sums = [None, None]
    own = dot(cols(me), integrals)
    pending = []
    held = pair
    last = n // 2
    for step in range(1, last + 1):
        owner = me + sign * step
        if step < last:
            held = lax.ppermute(held, ("row", "col"), ring)
            arrived = [(held, owner, None)]
        else:
            q = kb // 2
            held = lax.ppermute(lax.dynamic_slice_in_dim(held, core * q, q, axis=1),
                                ("row", "col"), ring)
            arrived = [(held, owner, q)]
        if step >= FIRST_DOT_STEP:
            for block, who, q in pending[:DOTS_PER_STEP]:
                a = cols(who)
                if q is not None:
                    a = lax.dynamic_slice_in_dim(a, core * q, q, axis=1)
                for k in range(2):
                    p = dot(a, block[k])
                    sums[k] = p if sums[k] is None else sums[k] + p
            pending = pending[DOTS_PER_STEP:]
            sums, held = lax.optimization_barrier((sums, held))
        pending = pending + arrived
    for block, who, q in pending:
        a = cols(who)
        if q is not None:
            a = lax.dynamic_slice_in_dim(a, core * q, q, axis=1)
        for k in range(2):
            p = dot(a, block[k])
            sums[k] = p if sums[k] is None else sums[k] + p

    mine = jnp.where(core == 0, sums[0], sums[1])
    theirs = jnp.where(core == 0, sums[1], sums[0])
    total = own + mine + lax.ppermute(theirs, "col", [(i, i ^ 1) for i in range(m)])

    mine = lax.dynamic_slice_in_dim(total, d * half, half, axis=0)
    other = lax.dynamic_slice_in_dim(total, (1 - d) * half, half, axis=0)
    other = lax.ppermute(other, "depth", [(0, 1), (1, 0)])
    return 0.5 * (mine + other)


def solution(mesh):
    placed = (P("row", ("col", "depth")), P(("row", "depth"), "col"))
    return jax.shard_map(
        local, mesh=mesh, in_specs=placed, out_specs=P(("row", "depth"), "col"), check_vma=False
    )
```

```python
import jax
import jax.numpy as jnp
from jax import lax
from jax.sharding import PartitionSpec as P


def ring_reduce(gathered, integrals, me, n):
    fwd = [(i, (i + 1) % n) for i in range(n)]
    bwd = [(i, (i - 1) % n) for i in range(n)]

    def part(t):
        block = lax.dynamic_index_in_dim(gathered, t % n, axis=0, keepdims=False)
        return jnp.dot(block, integrals, precision=lax.Precision.HIGHEST,
                       preferred_element_type=jnp.float32)

    back = n // 2
    ahead = n - 1 - back
    acc_f = part(me + ahead)
    acc_b = part(me - back)
    for s in range(1, back + 1):
        if s <= ahead:
            acc_f = lax.ppermute(acc_f, "row", fwd) + part(me + ahead - s)
        got = lax.ppermute(acc_b, "row", bwd)
        acc_b = got + part(me - back + s) if s < back else got
    return acc_f + acc_b


def local(amplitudes, integrals):
    n = lax.axis_size("row")
    me = lax.axis_index("row")
    d = lax.axis_index("depth")
    rows = amplitudes.shape[0]
    half = rows // 2

    swap = [(i * n + c, c * n + i) for i in range(n) for c in range(n)]
    moved = lax.ppermute(amplitudes, ("row", "col"), swap)
    gathered = lax.all_gather(moved, "col", axis=0, tiled=False)
    total = ring_reduce(gathered, integrals, me, n)

    mine = lax.dynamic_slice_in_dim(total, d * half, half, axis=0)
    other = lax.dynamic_slice_in_dim(total, (1 - d) * half, half, axis=0)
    other = lax.ppermute(other, "depth", [(0, 1), (1, 0)])
    return 0.5 * (mine + other)


def solution(mesh):
    placed = (P("row", ("col", "depth")), P(("row", "depth"), "col"))
    return jax.shard_map(
        local, mesh=mesh, in_specs=placed, out_specs=P(("row", "depth"), "col"), check_vma=False
    )
```

```python
import jax
import jax.numpy as jnp
from jax import lax
from jax.sharding import PartitionSpec as P

FIRST_DOT_STEP = 6
DOTS_PER_STEP = 6


def gather_col(block):
    n = lax.axis_size("col")
    c = lax.axis_index("col")
    core, xlo, y = c % 2, (c // 2) % 2, c // 4
    ny = n // 4
    other = lax.ppermute(block, "col", [(i, i ^ 1) for i in range(n)])
    pair = jnp.where(core == 0, jnp.stack([block, other]), jnp.stack([other, block]))
    far = lax.ppermute(pair, "col", [(i, i ^ 2) for i in range(n)])
    quad = jnp.where(xlo == 0, jnp.concatenate([pair, far]), jnp.concatenate([far, pair]))
    up = [(i, (i + 4) % n) for i in range(n)]
    down = [(i, (i - 4) % n) for i in range(n)]
    below = lax.ppermute(quad, "col", up)
    above = lax.ppermute(quad, "col", down)
    h = quad.shape[1] // 2
    opp_a = lax.ppermute(below[:, :h], "col", up)
    opp_b = lax.ppermute(above[:, h:], "col", down)
    opposite = jnp.concatenate([opp_a, opp_b], axis=1)
    stack = jnp.concatenate([quad, above, opposite, below])

    def place(owner):
        return ((owner // 4 - y) % ny) * 4 + owner % 4

    return stack, place


def local(amplitudes, integrals):
    n = lax.axis_size("row")
    me = lax.axis_index("row")
    d = lax.axis_index("depth")
    kb = integrals.shape[0]
    rows = amplitudes.shape[0]
    half = rows // 2

    strip, place = gather_col(amplitudes)

    def product(block, owner, lo=0, hi=None):
        hi = kb if hi is None else hi
        cols = lax.dynamic_index_in_dim(strip, place(owner), axis=0, keepdims=False)
        return jnp.dot(cols[:, lo:hi], block, precision=lax.Precision.HIGHEST,
                       preferred_element_type=jnp.float32)

    fwd = [(i, (i + 1) % n) for i in range(n)]
    bwd = [(i, (i - 1) % n) for i in range(n)]
    total = None
    pending = [(integrals, me, 0, kb)]
    ahead = integrals
    behind = integrals
    last = n // 2
    for step in range(1, last + 1):
        arrived = []
        if step < last:
            ahead = lax.ppermute(ahead, "row", fwd)
            arrived.append((ahead, (me - step) % n, 0, kb))
            behind = lax.ppermute(behind, "row", bwd)
            arrived.append((behind, (me + step) % n, 0, kb))
        else:
            m = kb // 2
            top = lax.ppermute(ahead[:m], "row", fwd)
            bottom = lax.ppermute(behind[m:], "row", bwd)
            arrived.append((top, (me - step) % n, 0, m))
            arrived.append((bottom, (me - step) % n, m, kb))
            ahead, behind = top, bottom
        if step >= FIRST_DOT_STEP:
            for block, owner, lo, hi in pending[:DOTS_PER_STEP]:
                part = product(block, owner, lo, hi)
                total = part if total is None else total + part
            pending = pending[DOTS_PER_STEP:]
            total, ahead, behind = lax.optimization_barrier((total, ahead, behind))
        pending = pending + arrived
    for block, owner, lo, hi in pending:
        part = product(block, owner, lo, hi)
        total = part if total is None else total + part

    mine = lax.dynamic_slice_in_dim(total, d * half, half, axis=0)
    other = lax.dynamic_slice_in_dim(total, (1 - d) * half, half, axis=0)
    other = lax.ppermute(other, "depth", [(0, 1), (1, 0)])
    return 0.5 * (mine + other)


def solution(mesh):
    placed = (P("row", ("col", "depth")), P(("row", "depth"), "col"))
    return jax.shard_map(
        local, mesh=mesh, in_specs=placed, out_specs=P(("row", "depth"), "col"), check_vma=False
    )
```

```python
import jax
import jax.numpy as jnp
from jax import lax
from jax.sharding import PartitionSpec as P

FIRST_DOT_STEP = 7
DOTS_PER_STEP = 8


def gather_col(block):
    n = lax.axis_size("col")
    c = lax.axis_index("col")
    core, xlo, y = c % 2, (c // 2) % 2, c // 4
    ny = n // 4
    other = lax.ppermute(block, "col", [(i, i ^ 1) for i in range(n)])
    pair = jnp.where(core == 0, jnp.stack([block, other]), jnp.stack([other, block]))
    far = lax.ppermute(pair, "col", [(i, i ^ 2) for i in range(n)])
    quad = jnp.where(xlo == 0, jnp.concatenate([pair, far]), jnp.concatenate([far, pair]))
    up = [(i, (i + 4) % n) for i in range(n)]
    down = [(i, (i - 4) % n) for i in range(n)]
    below = lax.ppermute(quad, "col", up)
    above = lax.ppermute(quad, "col", down)
    h = quad.shape[1] // 2
    opp_a = lax.ppermute(below[:, :h], "col", up)
    opp_b = lax.ppermute(above[:, h:], "col", down)
    opposite = jnp.concatenate([opp_a, opp_b], axis=1)
    stack = jnp.concatenate([quad, above, opposite, below])

    def place(owner):
        return ((owner // 4 - y) % ny) * 4 + owner % 4

    return stack, place


def local(amplitudes, integrals):
    n = lax.axis_size("row")
    me = lax.axis_index("row")
    d = lax.axis_index("depth")
    kb = integrals.shape[0]
    rows = amplitudes.shape[0]
    half = rows // 2

    fwd = [(i, (i + 1) % n) for i in range(n)]
    bwd = [(i, (i - 1) % n) for i in range(n)]
    first_ahead = lax.ppermute(integrals, "row", fwd)
    first_behind = lax.ppermute(integrals, "row", bwd)
    amplitudes, first_ahead, first_behind = lax.optimization_barrier(
        (amplitudes, first_ahead, first_behind))
    strip, place = gather_col(amplitudes)

    def product(block, owner, lo=0, hi=None):
        hi = kb if hi is None else hi
        cols = lax.dynamic_index_in_dim(strip, place(owner), axis=0, keepdims=False)
        return jnp.dot(cols[:, lo:hi], block, precision=lax.Precision.HIGHEST,
                       preferred_element_type=jnp.float32)

    total = None
    pending = [(integrals, me, 0, kb)]
    ahead = integrals
    behind = integrals
    last = n // 2
    for step in range(1, last + 1):
        arrived = []
        if step == 1:
            ahead, behind = first_ahead, first_behind
            arrived.append((ahead, (me - step) % n, 0, kb))
            arrived.append((behind, (me + step) % n, 0, kb))
        elif step < last:
            ahead = lax.ppermute(ahead, "row", fwd)
            arrived.append((ahead, (me - step) % n, 0, kb))
            behind = lax.ppermute(behind, "row", bwd)
            arrived.append((behind, (me + step) % n, 0, kb))
        else:
            m = kb // 2
            top = lax.ppermute(ahead[:m], "row", fwd)
            bottom = lax.ppermute(behind[m:], "row", bwd)
            arrived.append((top, (me - step) % n, 0, m))
            arrived.append((bottom, (me - step) % n, m, kb))
            ahead, behind = top, bottom
        if step >= FIRST_DOT_STEP:
            for block, owner, lo, hi in pending[:DOTS_PER_STEP]:
                part = product(block, owner, lo, hi)
                total = part if total is None else total + part
            pending = pending[DOTS_PER_STEP:]
            total, ahead, behind = lax.optimization_barrier((total, ahead, behind))
        pending = pending + arrived
    for block, owner, lo, hi in pending:
        part = product(block, owner, lo, hi)
        total = part if total is None else total + part

    mine = lax.dynamic_slice_in_dim(total, d * half, half, axis=0)
    other = lax.dynamic_slice_in_dim(total, (1 - d) * half, half, axis=0)
    other = lax.ppermute(other, "depth", [(0, 1), (1, 0)])
    return 0.5 * (mine + other)


def solution(mesh):
    placed = (P("row", ("col", "depth")), P(("row", "depth"), "col"))
    return jax.shard_map(
        local, mesh=mesh, in_specs=placed, out_specs=P(("row", "depth"), "col"), check_vma=False
    )
```

```python
import jax
import jax.numpy as jnp
from jax import lax
from jax.sharding import PartitionSpec as P

FIRST_DOT_STEP = 6
DOTS_PER_STEP = 6


def gather_col(block):
    n = lax.axis_size("col")
    c = lax.axis_index("col")
    core, xlo, y = c % 2, (c // 2) % 2, c // 4
    ny = n // 4
    other = lax.ppermute(block, "col", [(i, i ^ 1) for i in range(n)])
    pair = jnp.where(core == 0, jnp.stack([block, other]), jnp.stack([other, block]))
    far = lax.ppermute(pair, "col", [(i, i ^ 2) for i in range(n)])
    quad = jnp.where(xlo == 0, jnp.concatenate([pair, far]), jnp.concatenate([far, pair]))
    up = [(i, (i + 4) % n) for i in range(n)]
    down = [(i, (i - 4) % n) for i in range(n)]
    below = lax.ppermute(quad, "col", up)
    above = lax.ppermute(quad, "col", down)
    h = quad.shape[1] // 2
    opp_a = lax.ppermute(below[:, :h], "col", up)
    opp_b = lax.ppermute(above[:, h:], "col", down)
    opposite = jnp.concatenate([opp_a, opp_b], axis=1)
    stack = jnp.concatenate([quad, above, opposite, below])

    def place(owner):
        return ((owner // 4 - y) % ny) * 4 + owner % 4

    return stack, place


def local(amplitudes, integrals):
    n = lax.axis_size("row")
    me = lax.axis_index("row")
    d = lax.axis_index("depth")
    kb = integrals.shape[0]
    rows = amplitudes.shape[0]
    half = rows // 2

    strip = lax.all_gather(amplitudes, "col", axis=0, tiled=False)

    def place(owner):
        return owner

    def product(block, owner, lo=0, hi=None):
        hi = kb if hi is None else hi
        cols = lax.dynamic_index_in_dim(strip, place(owner), axis=0, keepdims=False)
        return jnp.dot(cols[:, lo:hi], block, precision=lax.Precision.HIGHEST,
                       preferred_element_type=jnp.float32)

    fwd = [(i, (i + 1) % n) for i in range(n)]
    bwd = [(i, (i - 1) % n) for i in range(n)]
    total = None
    pending = [(integrals, me, 0, kb)]
    ahead = integrals
    behind = integrals
    last = n // 2
    for step in range(1, last + 1):
        arrived = []
        if step < last:
            ahead = lax.ppermute(ahead, "row", fwd)
            arrived.append((ahead, (me - step) % n, 0, kb))
            behind = lax.ppermute(behind, "row", bwd)
            arrived.append((behind, (me + step) % n, 0, kb))
        else:
            m = kb // 2
            top = lax.ppermute(ahead[:m], "row", fwd)
            bottom = lax.ppermute(behind[m:], "row", bwd)
            arrived.append((top, (me - step) % n, 0, m))
            arrived.append((bottom, (me - step) % n, m, kb))
            ahead, behind = top, bottom
        if step >= FIRST_DOT_STEP:
            for block, owner, lo, hi in pending[:DOTS_PER_STEP]:
                part = product(block, owner, lo, hi)
                total = part if total is None else total + part
            pending = pending[DOTS_PER_STEP:]
            total, ahead, behind = lax.optimization_barrier((total, ahead, behind))
        pending = pending + arrived
    for block, owner, lo, hi in pending:
        part = product(block, owner, lo, hi)
        total = part if total is None else total + part

    mine = lax.dynamic_slice_in_dim(total, d * half, half, axis=0)
    other = lax.dynamic_slice_in_dim(total, (1 - d) * half, half, axis=0)
    other = lax.ppermute(other, "depth", [(0, 1), (1, 0)])
    return 0.5 * (mine + other)


def solution(mesh):
    placed = (P("row", ("col", "depth")), P(("row", "depth"), "col"))
    return jax.shard_map(
        local, mesh=mesh, in_specs=placed, out_specs=P(("row", "depth"), "col"), check_vma=False
    )
```

```python
import jax
import jax.numpy as jnp
from jax import lax
from jax.sharding import PartitionSpec as P

FIRST_DOT_STEP = 6
DOTS_PER_STEP = 6


def gather_col(block):
    n = lax.axis_size("col")
    c = lax.axis_index("col")
    core, xlo, y = c % 2, (c // 2) % 2, c // 4
    ny = n // 4
    up = [(i, (i + 4) % n) for i in range(n)]
    down = [(i, (i - 4) % n) for i in range(n)]
    below = lax.ppermute(block, "col", up)
    above = lax.ppermute(block, "col", down)
    h = block.shape[0] // 2
    opp_a = lax.ppermute(below[:h], "col", up)
    opp_b = lax.ppermute(above[h:], "col", down)
    opposite = jnp.concatenate([opp_a, opp_b], axis=0)
    ring = jnp.stack([block, above, opposite, below])
    far = lax.ppermute(ring, "col", [(i, i ^ 2) for i in range(n)])
    pair = jnp.where(xlo == 0, jnp.stack([ring, far]), jnp.stack([far, ring]))
    other = lax.ppermute(pair, "col", [(i, i ^ 1) for i in range(n)])
    quad = jnp.where(core == 0, jnp.stack([pair, other]), jnp.stack([other, pair]))
    stack = jnp.reshape(jnp.transpose(quad, (2, 1, 0, 3, 4)), (n,) + block.shape)

    def place(owner):
        return ((owner // 4 - y) % ny) * 4 + owner % 4

    return stack, place


def local(amplitudes, integrals):
    n = lax.axis_size("row")
    me = lax.axis_index("row")
    d = lax.axis_index("depth")
    kb = integrals.shape[0]
    rows = amplitudes.shape[0]
    half = rows // 2

    strip, place = gather_col(amplitudes)

    def product(block, owner, lo=0, hi=None):
        hi = kb if hi is None else hi
        cols = lax.dynamic_index_in_dim(strip, place(owner), axis=0, keepdims=False)
        return jnp.dot(cols[:, lo:hi], block, precision=lax.Precision.HIGHEST,
                       preferred_element_type=jnp.float32)

    fwd = [(i, (i + 1) % n) for i in range(n)]
    bwd = [(i, (i - 1) % n) for i in range(n)]
    total = None
    pending = [(integrals, me, 0, kb)]
    ahead = integrals
    behind = integrals
    last = n // 2
    for step in range(1, last + 1):
        arrived = []
        if step < last:
            ahead = lax.ppermute(ahead, "row", fwd)
            arrived.append((ahead, (me - step) % n, 0, kb))
            behind = lax.ppermute(behind, "row", bwd)
            arrived.append((behind, (me + step) % n, 0, kb))
        else:
            m = kb // 2
            top = lax.ppermute(ahead[:m], "row", fwd)
            bottom = lax.ppermute(behind[m:], "row", bwd)
            arrived.append((top, (me - step) % n, 0, m))
            arrived.append((bottom, (me - step) % n, m, kb))
            ahead, behind = top, bottom
        if step >= FIRST_DOT_STEP:
            for block, owner, lo, hi in pending[:DOTS_PER_STEP]:
                part = product(block, owner, lo, hi)
                total = part if total is None else total + part
            pending = pending[DOTS_PER_STEP:]
            total, ahead, behind = lax.optimization_barrier((total, ahead, behind))
        pending = pending + arrived
    for block, owner, lo, hi in pending:
        part = product(block, owner, lo, hi)
        total = part if total is None else total + part

    mine = lax.dynamic_slice_in_dim(total, d * half, half, axis=0)
    other = lax.dynamic_slice_in_dim(total, (1 - d) * half, half, axis=0)
    other = lax.ppermute(other, "depth", [(0, 1), (1, 0)])
    return 0.5 * (mine + other)


def solution(mesh):
    placed = (P("row", ("col", "depth")), P(("row", "depth"), "col"))
    return jax.shard_map(
        local, mesh=mesh, in_specs=placed, out_specs=P(("row", "depth"), "col"), check_vma=False
    )
```

```python
import jax
import jax.numpy as jnp
from jax import lax
from jax.sharding import PartitionSpec as P

FIRST_DOT_STEP = 4
DOTS_PER_STEP = 4


def gather_col(block):
    n = lax.axis_size("col")
    c = lax.axis_index("col")
    core, xlo, y = c % 2, (c // 2) % 2, c // 4
    ny = n // 4
    other = lax.ppermute(block, "col", [(i, i ^ 1) for i in range(n)])
    pair = jnp.where(core == 0, jnp.stack([block, other]), jnp.stack([other, block]))
    far = lax.ppermute(pair, "col", [(i, i ^ 2) for i in range(n)])
    quad = jnp.where(xlo == 0, jnp.concatenate([pair, far]), jnp.concatenate([far, pair]))
    up = [(i, (i + 4) % n) for i in range(n)]
    down = [(i, (i - 4) % n) for i in range(n)]
    below = lax.ppermute(quad, "col", up)
    above = lax.ppermute(quad, "col", down)
    h = quad.shape[1] // 2
    opp_a = lax.ppermute(below[:, :h], "col", up)
    opp_b = lax.ppermute(above[:, h:], "col", down)
    opposite = jnp.concatenate([opp_a, opp_b], axis=1)
    stack = jnp.concatenate([quad, above, opposite, below])

    def place(owner):
        return ((owner // 4 - y) % ny) * 4 + owner % 4

    return stack, place


def local(amplitudes, integrals):
    n = lax.axis_size("row")
    me = lax.axis_index("row")
    d = lax.axis_index("depth")
    kb = integrals.shape[0]
    rows = amplitudes.shape[0]
    half = rows // 2

    strip, place = gather_col(amplitudes)

    def product(block, owner, lo=0, hi=None):
        hi = kb if hi is None else hi
        cols = lax.dynamic_index_in_dim(strip, place(owner), axis=0, keepdims=False)
        return jnp.dot(cols[:, lo:hi], block, precision=lax.Precision.HIGHEST,
                       preferred_element_type=jnp.float32)

    fwd = [(i, (i + 1) % n) for i in range(n)]
    bwd = [(i, (i - 1) % n) for i in range(n)]
    total = None
    pending = [(integrals, me, 0, kb)]
    ahead = integrals
    behind = integrals
    last = n // 2
    for step in range(1, last + 1):
        arrived = []
        if step < last:
            ahead = lax.ppermute(ahead, "row", fwd)
            arrived.append((ahead, (me - step) % n, 0, kb))
            behind = lax.ppermute(behind, "row", bwd)
            arrived.append((behind, (me + step) % n, 0, kb))
        else:
            m = kb // 2
            top = lax.ppermute(ahead[:m], "row", fwd)
            bottom = lax.ppermute(behind[m:], "row", bwd)
            arrived.append((top, (me - step) % n, 0, m))
            arrived.append((bottom, (me - step) % n, m, kb))
            ahead, behind = top, bottom
        if step >= FIRST_DOT_STEP:
            for block, owner, lo, hi in pending[:DOTS_PER_STEP]:
                part = product(block, owner, lo, hi)
                total = part if total is None else total + part
            pending = pending[DOTS_PER_STEP:]
            total, ahead, behind = lax.optimization_barrier((total, ahead, behind))
        pending = pending + arrived
    for block, owner, lo, hi in pending:
        part = product(block, owner, lo, hi)
        total = part if total is None else total + part

    mine = lax.dynamic_slice_in_dim(total, d * half, half, axis=0)
    other = lax.dynamic_slice_in_dim(total, (1 - d) * half, half, axis=0)
    other = lax.ppermute(other, "depth", [(0, 1), (1, 0)])
    return 0.5 * (mine + other)


def solution(mesh):
    placed = (P("row", ("col", "depth")), P(("row", "depth"), "col"))
    return jax.shard_map(
        local, mesh=mesh, in_specs=placed, out_specs=P(("row", "depth"), "col"), check_vma=False
    )
```

```python
import jax
import jax.numpy as jnp
from jax import lax
from jax.sharding import PartitionSpec as P

FIRST_DOT_STEP = 6
DOTS_PER_STEP = 6


def gather_col(block):
    n = lax.axis_size("col")
    c = lax.axis_index("col")
    core, xlo, y = c % 2, (c // 2) % 2, c // 4
    ny = n // 4
    other = lax.ppermute(block, "col", [(i, i ^ 1) for i in range(n)])
    pair = jnp.where(core == 0, jnp.stack([block, other]), jnp.stack([other, block]))
    far = lax.ppermute(pair, "col", [(i, i ^ 2) for i in range(n)])
    quad = jnp.where(xlo == 0, jnp.concatenate([pair, far]), jnp.concatenate([far, pair]))
    up = [(i, (i + 4) % n) for i in range(n)]
    down = [(i, (i - 4) % n) for i in range(n)]
    below = lax.ppermute(quad, "col", up)
    above = lax.ppermute(quad, "col", down)
    h = quad.shape[1] // 2
    opp_a = lax.ppermute(below[:, :h], "col", up)
    opp_b = lax.ppermute(above[:, h:], "col", down)
    opposite = jnp.concatenate([opp_a, opp_b], axis=1)
    stack = jnp.concatenate([quad, above, opposite, below])

    def place(owner):
        return ((owner // 4 - y) % ny) * 4 + owner % 4

    return stack, place


def local(amplitudes, integrals):
    n = lax.axis_size("row")
    me = lax.axis_index("row")
    d = lax.axis_index("depth")
    kb = integrals.shape[0]
    rows = amplitudes.shape[0]
    half = rows // 2

    strip, place = gather_col(amplitudes)

    def product(block, owner, lo=0, hi=None, start=None):
        hi = kb if hi is None else hi
        cols = lax.dynamic_index_in_dim(strip, place(owner), axis=0, keepdims=False)
        if start is not None:
            cols = lax.dynamic_slice_in_dim(cols, start, half, axis=0)
        return jnp.dot(cols[:, lo:hi], block, precision=lax.Precision.HIGHEST,
                       preferred_element_type=jnp.float32)

    fwd = [(i, (i + 1) % n) for i in range(n)]
    bwd = [(i, (i - 1) % n) for i in range(n)]
    total = None
    pending = [(integrals, me, 0, kb)]
    ahead = integrals
    behind = integrals
    last = n // 2
    for step in range(1, last + 1):
        arrived = []
        if step < last:
            ahead = lax.ppermute(ahead, "row", fwd)
            arrived.append((ahead, (me - step) % n, 0, kb))
            behind = lax.ppermute(behind, "row", bwd)
            arrived.append((behind, (me + step) % n, 0, kb))
        else:
            m = kb // 2
            top = lax.ppermute(ahead[:m], "row", fwd)
            bottom = lax.ppermute(behind[m:], "row", bwd)
            arrived.append((top, (me - step) % n, 0, m))
            arrived.append((bottom, (me - step) % n, m, kb))
            ahead, behind = top, bottom
        if step >= FIRST_DOT_STEP:
            for block, owner, lo, hi in pending[:DOTS_PER_STEP]:
                part = product(block, owner, lo, hi)
                total = part if total is None else total + part
            pending = pending[DOTS_PER_STEP:]
            total, ahead, behind = lax.optimization_barrier((total, ahead, behind))
        pending = pending + arrived
    mine = lax.dynamic_slice_in_dim(total, d * half, half, axis=0)
    other = lax.dynamic_slice_in_dim(total, (1 - d) * half, half, axis=0)
    for block, owner, lo, hi in pending:
        other = other + product(block, owner, lo, hi, (1 - d) * half)
    other = lax.ppermute(other, "depth", [(0, 1), (1, 0)])
    for block, owner, lo, hi in pending:
        mine = mine + product(block, owner, lo, hi, d * half)
    return 0.5 * (mine + other)


def solution(mesh):
    placed = (P("row", ("col", "depth")), P(("row", "depth"), "col"))
    return jax.shard_map(
        local, mesh=mesh, in_specs=placed, out_specs=P(("row", "depth"), "col"), check_vma=False
    )
```

```python
import jax
import jax.numpy as jnp
from jax import lax
from jax.sharding import PartitionSpec as P

FIRST_DOT_STEP = 6
DOTS_PER_STEP = 5


def gather_col(block):
    n = lax.axis_size("col")
    c = lax.axis_index("col")
    core, xlo, y = c % 2, (c // 2) % 2, c // 4
    ny = n // 4
    other = lax.ppermute(block, "col", [(i, i ^ 1) for i in range(n)])
    pair = jnp.where(core == 0, jnp.stack([block, other]), jnp.stack([other, block]))
    far = lax.ppermute(pair, "col", [(i, i ^ 2) for i in range(n)])
    quad = jnp.where(xlo == 0, jnp.concatenate([pair, far]), jnp.concatenate([far, pair]))
    up = [(i, (i + 4) % n) for i in range(n)]
    down = [(i, (i - 4) % n) for i in range(n)]
    below = lax.ppermute(quad, "col", up)
    above = lax.ppermute(quad, "col", down)
    h = quad.shape[1] // 2
    opp_a = lax.ppermute(below[:, :h], "col", up)
    opp_b = lax.ppermute(above[:, h:], "col", down)
    opposite = jnp.concatenate([opp_a, opp_b], axis=1)
    stack = jnp.concatenate([quad, above, opposite, below])

    def place(owner):
        return ((owner // 4 - y) % ny) * 4 + owner % 4

    return stack, place


def local(amplitudes, integrals):
    n = lax.axis_size("row")
    me = lax.axis_index("row")
    d = lax.axis_index("depth")
    kb = integrals.shape[0]
    rows = amplitudes.shape[0]
    half = rows // 2

    strip, place = gather_col(amplitudes)

    def product(block, owner, lo=0, hi=None, start=None):
        hi = kb if hi is None else hi
        cols = lax.dynamic_index_in_dim(strip, place(owner), axis=0, keepdims=False)
        if start is not None:
            cols = lax.dynamic_slice_in_dim(cols, start, half, axis=0)
        return jnp.dot(cols[:, lo:hi], block, precision=lax.Precision.HIGHEST,
                       preferred_element_type=jnp.float32)

    fwd = [(i, (i + 1) % n) for i in range(n)]
    bwd = [(i, (i - 1) % n) for i in range(n)]
    total = None
    pending = [(integrals, me, 0, kb)]
    ahead = integrals
    behind = integrals
    last = n // 2
    for step in range(1, last + 1):
        arrived = []
        if step < last:
            ahead = lax.ppermute(ahead, "row", fwd)
            arrived.append((ahead, (me - step) % n, 0, kb))
            behind = lax.ppermute(behind, "row", bwd)
            arrived.append((behind, (me + step) % n, 0, kb))
        else:
            m = kb // 2
            top = lax.ppermute(ahead[:m], "row", fwd)
            bottom = lax.ppermute(behind[m:], "row", bwd)
            arrived.append((top, (me - step) % n, 0, m))
            arrived.append((bottom, (me - step) % n, m, kb))
            ahead, behind = top, bottom
        if step >= FIRST_DOT_STEP:
            for block, owner, lo, hi in pending[:DOTS_PER_STEP]:
                part = product(block, owner, lo, hi)
                total = part if total is None else total + part
            pending = pending[DOTS_PER_STEP:]
            total, ahead, behind = lax.optimization_barrier((total, ahead, behind))
        pending = pending + arrived
    mine = lax.dynamic_slice_in_dim(total, d * half, half, axis=0)
    other = lax.dynamic_slice_in_dim(total, (1 - d) * half, half, axis=0)
    for block, owner, lo, hi in pending:
        other = other + product(block, owner, lo, hi, (1 - d) * half)
    other = lax.ppermute(other, "depth", [(0, 1), (1, 0)])
    for block, owner, lo, hi in pending:
        mine = mine + product(block, owner, lo, hi, d * half)
    return 0.5 * (mine + other)


def solution(mesh):
    placed = (P("row", ("col", "depth")), P(("row", "depth"), "col"))
    return jax.shard_map(
        local, mesh=mesh, in_specs=placed, out_specs=P(("row", "depth"), "col"), check_vma=False
    )
```

```python
import jax
import jax.numpy as jnp
from jax import lax
from jax.sharding import PartitionSpec as P

FIRST_DOT_STEP = 6
DOTS_PER_STEP = 6


def gather_col(block):
    n = lax.axis_size("col")
    c = lax.axis_index("col")
    core, xlo, y = c % 2, (c // 2) % 2, c // 4
    ny = n // 4
    other = lax.ppermute(block, "col", [(i, i ^ 1) for i in range(n)])
    pair = jnp.where(core == 0, jnp.stack([block, other]), jnp.stack([other, block]))
    far = lax.ppermute(pair, "col", [(i, i ^ 2) for i in range(n)])
    quad = jnp.where(xlo == 0, jnp.concatenate([pair, far]), jnp.concatenate([far, pair]))
    up = [(i, (i + 4) % n) for i in range(n)]
    down = [(i, (i - 4) % n) for i in range(n)]
    below = lax.ppermute(quad, "col", up)
    above = lax.ppermute(quad, "col", down)
    h = quad.shape[1] // 2
    opp_a = lax.ppermute(below[:, :h], "col", up)
    opp_b = lax.ppermute(above[:, h:], "col", down)
    opposite = jnp.concatenate([opp_a, opp_b], axis=1)
    stack = jnp.concatenate([quad, above, opposite, below])

    def place(owner):
        return ((owner // 4 - y) % ny) * 4 + owner % 4

    return stack, place


def local(amplitudes, integrals):
    n = lax.axis_size("row")
    me = lax.axis_index("row")
    d = lax.axis_index("depth")
    kb = integrals.shape[0]
    rows = amplitudes.shape[0]
    half = rows // 2

    strip, place = gather_col(amplitudes)

    def product(block, owner, lo=0, hi=None, start=None):
        hi = kb if hi is None else hi
        cols = lax.dynamic_index_in_dim(strip, place(owner), axis=0, keepdims=False)
        if start is not None:
            cols = lax.dynamic_slice_in_dim(cols, start, half, axis=0)
        return jnp.dot(cols[:, lo:hi], block, precision=lax.Precision.HIGHEST,
                       preferred_element_type=jnp.float32)

    fwd = [(i, (i + 1) % n) for i in range(n)]
    bwd = [(i, (i - 1) % n) for i in range(n)]
    total = None
    pending = [(integrals, me, 0, kb)]
    ahead = integrals
    behind = integrals
    last = n // 2
    for step in range(1, last + 1):
        arrived = []
        if step < last:
            ahead = lax.ppermute(ahead, "row", fwd)
            arrived.append((ahead, (me - step) % n, 0, kb))
            behind = lax.ppermute(behind, "row", bwd)
            arrived.append((behind, (me + step) % n, 0, kb))
        else:
            m = kb // 2
            top = lax.ppermute(ahead[:m], "row", fwd)
            bottom = lax.ppermute(behind[m:], "row", bwd)
            arrived.append((top, (me - step) % n, 0, m))
            arrived.append((bottom, (me - step) % n, m, kb))
            ahead, behind = top, bottom
        if step == FIRST_DOT_STEP - 1:
            strip, ahead, behind = lax.optimization_barrier((strip, ahead, behind))
        if step >= FIRST_DOT_STEP:
            for block, owner, lo, hi in pending[:DOTS_PER_STEP]:
                part = product(block, owner, lo, hi)
                total = part if total is None else total + part
            pending = pending[DOTS_PER_STEP:]
            total, ahead, behind = lax.optimization_barrier((total, ahead, behind))
        pending = pending + arrived
    mine = lax.dynamic_slice_in_dim(total, d * half, half, axis=0)
    other = lax.dynamic_slice_in_dim(total, (1 - d) * half, half, axis=0)
    for block, owner, lo, hi in pending:
        other = other + product(block, owner, lo, hi, (1 - d) * half)
    other = lax.ppermute(other, "depth", [(0, 1), (1, 0)])
    for block, owner, lo, hi in pending:
        mine = mine + product(block, owner, lo, hi, d * half)
    return 0.5 * (mine + other)


def solution(mesh):
    placed = (P("row", ("col", "depth")), P(("row", "depth"), "col"))
    return jax.shard_map(
        local, mesh=mesh, in_specs=placed, out_specs=P(("row", "depth"), "col"), check_vma=False
    )
```

```python
import jax
import jax.numpy as jnp
from jax import lax
from jax.sharding import PartitionSpec as P

FIRST_DOT_STEP = 6
DOTS_PER_STEP = 7


def gather_col(block):
    n = lax.axis_size("col")
    c = lax.axis_index("col")
    core, xlo, y = c % 2, (c // 2) % 2, c // 4
    ny = n // 4
    other = lax.ppermute(block, "col", [(i, i ^ 1) for i in range(n)])
    pair = jnp.where(core == 0, jnp.stack([block, other]), jnp.stack([other, block]))
    far = lax.ppermute(pair, "col", [(i, i ^ 2) for i in range(n)])
    quad = jnp.where(xlo == 0, jnp.concatenate([pair, far]), jnp.concatenate([far, pair]))
    up = [(i, (i + 4) % n) for i in range(n)]
    down = [(i, (i - 4) % n) for i in range(n)]
    below = lax.ppermute(quad, "col", up)
    above = lax.ppermute(quad, "col", down)
    h = quad.shape[1] // 2
    opp_a = lax.ppermute(below[:, :h], "col", up)
    opp_b = lax.ppermute(above[:, h:], "col", down)
    opposite = jnp.concatenate([opp_a, opp_b], axis=1)
    stack = jnp.concatenate([quad, above, opposite, below])

    def place(owner):
        return ((owner // 4 - y) % ny) * 4 + owner % 4

    return stack, place


def local(amplitudes, integrals):
    n = lax.axis_size("row")
    me = lax.axis_index("row")
    d = lax.axis_index("depth")
    kb = integrals.shape[0]
    rows = amplitudes.shape[0]
    half = rows // 2

    strip, place = gather_col(amplitudes)

    def product(block, owner, lo=0, hi=None, start=None):
        hi = kb if hi is None else hi
        cols = lax.dynamic_index_in_dim(strip, place(owner), axis=0, keepdims=False)
        if start is not None:
            cols = lax.dynamic_slice_in_dim(cols, start, half, axis=0)
        return jnp.dot(cols[:, lo:hi], block, precision=lax.Precision.HIGHEST,
                       preferred_element_type=jnp.float32)

    fwd = [(i, (i + 1) % n) for i in range(n)]
    bwd = [(i, (i - 1) % n) for i in range(n)]
    total = None
    pending = [(integrals, me, 0, kb)]
    ahead = integrals
    behind = integrals
    last = n // 2
    for step in range(1, last + 1):
        arrived = []
        if step < last:
            ahead = lax.ppermute(ahead, "row", fwd)
            arrived.append((ahead, (me - step) % n, 0, kb))
            behind = lax.ppermute(behind, "row", bwd)
            arrived.append((behind, (me + step) % n, 0, kb))
        else:
            m = kb // 2
            top = lax.ppermute(ahead[:m], "row", fwd)
            bottom = lax.ppermute(behind[m:], "row", bwd)
            arrived.append((top, (me - step) % n, 0, m))
            arrived.append((bottom, (me - step) % n, m, kb))
            ahead, behind = top, bottom
        if step == FIRST_DOT_STEP - 1:
            strip, ahead, behind = lax.optimization_barrier((strip, ahead, behind))
        if step >= FIRST_DOT_STEP:
            for block, owner, lo, hi in pending[:DOTS_PER_STEP]:
                part = product(block, owner, lo, hi)
                total = part if total is None else total + part
            pending = pending[DOTS_PER_STEP:]
            total, ahead, behind = lax.optimization_barrier((total, ahead, behind))
        pending = pending + arrived
    mine = lax.dynamic_slice_in_dim(total, d * half, half, axis=0)
    other = lax.dynamic_slice_in_dim(total, (1 - d) * half, half, axis=0)
    for block, owner, lo, hi in pending:
        other = other + product(block, owner, lo, hi, (1 - d) * half)
    other = lax.ppermute(other, "depth", [(0, 1), (1, 0)])
    for block, owner, lo, hi in pending:
        mine = mine + product(block, owner, lo, hi, d * half)
    return 0.5 * (mine + other)


def solution(mesh):
    placed = (P("row", ("col", "depth")), P(("row", "depth"), "col"))
    return jax.shard_map(
        local, mesh=mesh, in_specs=placed, out_specs=P(("row", "depth"), "col"), check_vma=False
    )
```

```python
import jax
import jax.numpy as jnp
from jax import lax
from jax.sharding import PartitionSpec as P

FIRST_DOT_STEP = 5
DOTS_AT_STEP = {5: 2, 6: 5, 7: 5, 8: 3}


def gather_col(block):
    n = lax.axis_size("col")
    c = lax.axis_index("col")
    core, xlo, y = c % 2, (c // 2) % 2, c // 4
    ny = n // 4
    other = lax.ppermute(block, "col", [(i, i ^ 1) for i in range(n)])
    pair = jnp.where(core == 0, jnp.stack([block, other]), jnp.stack([other, block]))
    far = lax.ppermute(pair, "col", [(i, i ^ 2) for i in range(n)])
    quad = jnp.where(xlo == 0, jnp.concatenate([pair, far]), jnp.concatenate([far, pair]))
    up = [(i, (i + 4) % n) for i in range(n)]
    down = [(i, (i - 4) % n) for i in range(n)]
    below = lax.ppermute(quad, "col", up)
    above = lax.ppermute(quad, "col", down)
    h = quad.shape[1] // 2
    opp_a = lax.ppermute(below[:, :h], "col", up)
    opp_b = lax.ppermute(above[:, h:], "col", down)
    opposite = jnp.concatenate([opp_a, opp_b], axis=1)
    stack = jnp.concatenate([quad, above, opposite, below])

    def place(owner):
        return ((owner // 4 - y) % ny) * 4 + owner % 4

    return stack, place


def local(amplitudes, integrals):
    n = lax.axis_size("row")
    me = lax.axis_index("row")
    d = lax.axis_index("depth")
    kb = integrals.shape[0]
    rows = amplitudes.shape[0]
    half = rows // 2

    strip, place = gather_col(amplitudes)

    def product(block, owner, lo=0, hi=None, start=None):
        hi = kb if hi is None else hi
        cols = lax.dynamic_index_in_dim(strip, place(owner), axis=0, keepdims=False)
        if start is not None:
            cols = lax.dynamic_slice_in_dim(cols, start, half, axis=0)
        return jnp.dot(cols[:, lo:hi], block, precision=lax.Precision.HIGHEST,
                       preferred_element_type=jnp.float32)

    fwd = [(i, (i + 1) % n) for i in range(n)]
    bwd = [(i, (i - 1) % n) for i in range(n)]
    total = None
    pending = [(integrals, me, 0, kb)]
    ahead = integrals
    behind = integrals
    last = n // 2
    for step in range(1, last + 1):
        arrived = []
        if step < last:
            ahead = lax.ppermute(ahead, "row", fwd)
            arrived.append((ahead, (me - step) % n, 0, kb))
            behind = lax.ppermute(behind, "row", bwd)
            arrived.append((behind, (me + step) % n, 0, kb))
        else:
            m = kb // 2
            top = lax.ppermute(ahead[:m], "row", fwd)
            bottom = lax.ppermute(behind[m:], "row", bwd)
            arrived.append((top, (me - step) % n, 0, m))
            arrived.append((bottom, (me - step) % n, m, kb))
            ahead, behind = top, bottom
        if step >= FIRST_DOT_STEP:
            count = DOTS_AT_STEP[step]
            for block, owner, lo, hi in pending[:count]:
                part = product(block, owner, lo, hi)
                total = part if total is None else total + part
            pending = pending[count:]
            total, ahead, behind = lax.optimization_barrier((total, ahead, behind))
        pending = pending + arrived
    mine = lax.dynamic_slice_in_dim(total, d * half, half, axis=0)
    other = lax.dynamic_slice_in_dim(total, (1 - d) * half, half, axis=0)
    for block, owner, lo, hi in pending:
        other = other + product(block, owner, lo, hi, (1 - d) * half)
    other = lax.ppermute(other, "depth", [(0, 1), (1, 0)])
    for block, owner, lo, hi in pending:
        mine = mine + product(block, owner, lo, hi, d * half)
    return 0.5 * (mine + other)


def solution(mesh):
    placed = (P("row", ("col", "depth")), P(("row", "depth"), "col"))
    return jax.shard_map(
        local, mesh=mesh, in_specs=placed, out_specs=P(("row", "depth"), "col"), check_vma=False
    )
```
